32 devices in a mesh: elem: 16 (over z, x, core), mode: 2 (over y).
Axes of the slice: x: 2, y: 2, z: 4, core: 2. Of those that a mesh axis runs over, the one named last changes fastest.
Arguments:
- velocity: float32 [1024, 128, 128], P(None, ('elem', 'mode')), may hold values from -6 to 6
- previous: float32 [1024, 128, 128], P('mode', 'elem'), may hold values from -6 to 6
- derivative: float32 [128, 128], replicated, may hold values from -0.5 to 0.5
- stiffness: float32 [128, 128], replicated, as said below
- coupling: float32 [4, 128, 128], replicated, may hold values from -0.25 to 0.25
- reaction: float32 [128], P('elem'), may hold values from 0.5 to 4
- axial_weight: float32 [128], P('elem'), may hold values from 0.5 to 4
- neighbours: int32 [128, 4], P('elem'), may hold values from -1 to 127, as said below
Outputs:
- solution: float32 [1024, 128, 128], P('mode', 'elem')
The draws below stay inside these ranges and needn't reach their ends.
Inputs may be any that keep to these rules, and one draw needn't show every extreme that they name: `stiffness`: symmetric with a positive diagonal. `neighbours`: elements lie on a grid of 2 rows, periodic along the rows, and 4 columns a group of 8 elements, groups in order along the columns with walls at both ends. A group's first 2 elements form its first column and its last 2 its last column; a neighbour in another group is in the next or previous group, among its first or last 2 elements.
All inputs are finite; a program needn't handle non-finite values.
Results may differ from the reference program's by a relative error of at most 0.0001.
Values sent between devices are 32-bit elements; how exact they have to be, the bound alone decides.
A program may use at most 128 MiB of HBM per device.

```python
import math
import jax
import jax.numpy as jnp
from jax import lax

Q = 128
NZ = 1024
EG = 8
EY = 2
E = 128


def draw_stiffness(key, part):
    first_key, second_key = jax.random.split(jax.random.fold_in(key, 11))
    diagonal = jax.random.uniform(first_key, (Q,), jnp.float32, 2.0, 6.0)
    noise = jax.random.normal(second_key, (Q, Q), jnp.float32) * (0.3 / math.sqrt(Q))
    return jnp.diag(diagonal) + 0.5 * (noise + noise.T)


def draw_neighbours(key, part):
    groups = E // EG
    columns = EG // EY
    places = jnp.arange(EG, dtype=jnp.int32)
    column_of = places // EY
    column_kind = jnp.where(column_of == 0, 0, jnp.where(column_of == columns - 1, 2, 1)).astype(jnp.int32)

    def arrange(group_index):
        shuffle = jax.random.permutation(jax.random.fold_in(jax.random.fold_in(key, 23), group_index), EG).astype(jnp.int32)
        slot_place = jnp.argsort(column_kind * EG + shuffle, stable=True).astype(jnp.int32)
        place_slot = jnp.argsort(slot_place, stable=True).astype(jnp.int32)
        return (slot_place, place_slot)
    orders, slots = jax.vmap(arrange)(jnp.arange(groups, dtype=jnp.int32))
    element_place = orders.reshape(-1)
    group_of = jnp.arange(E, dtype=jnp.int32) // EG
    grid_col = group_of * columns + element_place // EY
    grid_row = element_place % EY
    total_cols = groups * columns

    def element_at(column_at, row_at):
        group_at = column_at // columns
        place_at = column_at % columns * EY + row_at
        return group_at * EG + slots[group_at, place_at]
    left_id = jnp.where(grid_col > 0, element_at(jnp.maximum(grid_col - 1, 0), grid_row), -1)
    right_id = jnp.where(grid_col < total_cols - 1, element_at(jnp.minimum(grid_col + 1, total_cols - 1), grid_row), -1)
    down_id = element_at(grid_col, (grid_row + EY - 1) % EY)
    up_id = element_at(grid_col, (grid_row + 1) % EY)
    return jnp.stack([left_id, right_id, down_id, up_id], axis=1).astype(jnp.int32)


def block_scale(key, dims, cuts, smallest, top_value):
    gain, own = 1.0, jax.random.fold_in(key, 6)
    for dim, parts in cuts:
        heights = jnp.exp(jax.random.uniform(jax.random.fold_in(own, dim), (parts,), jnp.float32, smallest / len(cuts), top_value / len(cuts)))
        gain = gain * jnp.repeat(heights, dims[dim] // parts).reshape([-1 if axis == dim else 1 for axis in range(len(dims))])
    return gain


def normal_values(rng, extent, width, most, cuts=(), kind=jnp.bfloat16):
    array = jax.random.normal(rng, extent, jnp.float32) * width
    if len(cuts) > 0:
        array = block_scale(rng, extent, cuts, -0.22, 0.18) * array
    return jnp.clip(array, min=-most, max=most).astype(kind)


def setup_inputs(seed: int = 0) -> dict:
    key_of = jax.random.split(jax.random.key(seed), 9)
    velocity = normal_values(key_of[0], (NZ, E, Q), 1.0, 6.0, ((1, 32),), jnp.float32)
    previous = normal_values(key_of[1], (NZ, E, Q), 1.0, 6.0, ((0, 2), (1, 16)), jnp.float32)
    derivative = normal_values(key_of[2], (Q, Q), Q ** -0.5, 0.5, (), jnp.float32)
    stiffness = draw_stiffness(jax.random.fold_in(key_of[8], 71), 0)
    coupling = normal_values(key_of[4], (4, Q, Q), (4 * Q) ** -0.5, 0.25, (), jnp.float32)
    reaction = jnp.clip(jnp.exp(math.log(4.0) - 2.0794415 * jax.random.uniform(key_of[5], (E,), jnp.float32) ** block_scale(key_of[5], (E,), ((0, 16),), -0.2, 0.2)), 0.5, 4.0)
    axial_weight = jnp.clip(jnp.exp(math.log(4.0) - 2.0794415 * jax.random.uniform(key_of[6], (E,), jnp.float32) ** block_scale(key_of[6], (E,), ((0, 16),), -0.2, 0.2)), 0.5, 4.0)
    neighbours = draw_neighbours(jax.random.fold_in(key_of[8], 71), 0)
    return dict(velocity=velocity, previous=previous, derivative=derivative, stiffness=stiffness, coupling=coupling, reaction=reaction, axial_weight=axial_weight, neighbours=neighbours)


highest = lax.Precision.HIGHEST
dt_step = 0.5
first_weight = 0.7
second_weight = 1.1


def row_shift(count):
    rows = jnp.arange(count, dtype=jnp.int32)
    half = count // 2
    waves = jnp.where(rows <= half, rows, rows - half).astype(jnp.float32)
    return 4.0 * (waves / half) ** 2


def reference(velocity, previous, derivative, stiffness, coupling, reaction, axial_weight, neighbours):
    slope = jnp.einsum('zeq,pq->zep', velocity, derivative, precision=highest)
    product = velocity - dt_step * velocity * slope
    spectrum = jnp.fft.rfft(product, axis=0)
    half = NZ // 2
    rhs = jnp.concatenate([spectrum.real[:half], spectrum.real[half:half + 1], spectrum.imag[1:half]], axis=0) * (NZ ** -0.5)
    shifts = row_shift(NZ).astype(rhs.dtype)
    present = neighbours >= 0
    near_index = jnp.where(present, neighbours, 0).astype(jnp.int32)
    face_mask = present.astype(rhs.dtype)
    stiff_diag = jnp.diagonal(stiffness)

    def apply(field, shift_rows):
        result = jnp.einsum('req,pq->rep', field, stiffness, precision=highest)
        result = result + (reaction[None, :, None] + shift_rows[:, None, None] * axial_weight[None, :, None]) * field
        for side_index in range(4):
            beside = jnp.take(field, near_index[:, side_index], axis=1) * face_mask[None, :, side_index, None]
            result = result + jnp.einsum('req,pq->rep', beside, coupling[side_index], precision=highest)
        return result

    def sweep_block(inputs):
        rhs_rows, start_rows, shift_rows = inputs
        inverse = 1.0 / (stiff_diag[None, None, :] + reaction[None, :, None] + shift_rows[:, None, None] * axial_weight[None, :, None])
        first = start_rows + first_weight * inverse * (rhs_rows - apply(start_rows, shift_rows))
        return first + second_weight * inverse * (rhs_rows - apply(first, shift_rows))

    blocks = 16
    rows_block = NZ // blocks
    result = lax.map(sweep_block, (rhs.reshape(blocks, rows_block, E, Q), previous.reshape(blocks, rows_block, E, Q), shifts.reshape(blocks, rows_block)))
    return result.reshape(NZ, E, Q)
```

```python
import functools
import math

import jax
import jax.numpy as jnp
import ml_dtypes
import numpy as np
from jax import lax
from jax.experimental import pallas as pl
from jax.experimental.pallas import tpu as pltpu
from jax.sharding import PartitionSpec as P

dt_step = 0.5
first_weight = 0.7
second_weight = 1.1
CHUNKS = 8
LAG = 2
MESH = pl.DeviceIdType.MESH
bf16 = jnp.bfloat16
f32 = jnp.float32


def dft_tables(planes, modes):
    half = planes // 2
    rows = np.arange(planes)
    waves = np.where(rows <= half, rows, rows - half)
    phase = (waves[:, None] * np.arange(half)[None, :]) % planes
    angles = 2.0 * math.pi / planes * phase
    table = np.where((rows <= half)[:, None], np.cos(angles), -np.sin(angles)) * planes ** (-0.5)
    table = table.reshape(modes, planes // modes // 2, 2, half).transpose(0, 2, 1, 3)
    high = table.astype(ml_dtypes.bfloat16)
    low = (table - high.astype(np.float64)).astype(ml_dtypes.bfloat16)
    return np.stack([high, low])


def split(values):
    high = values.astype(bf16)
    low = (values - high.astype(f32)).astype(bf16)
    return high, low


def kernel(
    modes, groups, planes, elems, group_elems, rows, nodes,
    vel_hbm, prev_hbm, table_hbm, der_hbm, stiff_hbm, coup_hbm, reac, axial, near,
    out_hbm,
    vel, prev, table, der, stiff, coup, w_slope, w_apply, folded, sent, rhs, rims, first,
    halo_prev, halo_first, pairs, staged, outv,
    load_sem, y_send, y_recv, p_send, p_recv, f_send, f_recv, out_sem,
):
    half = planes // 2
    rim = group_elems // 4
    count = rows // CHUNKS
    me = lax.axis_index("mode")
    group = lax.axis_index("elem")
    zero_slot = group_elems + 2 * rim

    loads = [
        pltpu.make_async_copy(src, dst, load_sem.at[i])
        for i, (src, dst) in enumerate(
            [
                (prev_hbm, prev), (vel_hbm, vel), (der_hbm, der), (table_hbm, table),
                (stiff_hbm, stiff), (coup_hbm, coup),
            ]
        )
    ]
    for load in loads:
        load.start()

    barrier = pltpu.get_barrier_semaphore()
    for step in range(1, modes):
        pl.semaphore_signal(
            barrier, inc=1, device_id={"mode": lax.rem(me + step, modes)}, device_id_type=MESH
        )
    has_left = group > 0
    has_right = group < groups - 1

    @pl.when(has_left)
    def _():
        pl.semaphore_signal(barrier, inc=1, device_id={"elem": group - 1}, device_id_type=MESH)

    @pl.when(has_right)
    def _():
        pl.semaphore_signal(barrier, inc=1, device_id={"elem": group + 1}, device_id_type=MESH)

    def start_row(c):
        return (2 * (c // 2) * count + c % 2) * group_elems

    def prev_rows(c, e):
        return prev[pl.ds(start_row(c) + e, count, stride=2 * group_elems), :]

    def halo_copies(source, halo, send, recv, c):
        right = pltpu.make_async_remote_copy(
            source(c, 0), halo.at[0, c], send.at[0, c], recv.at[0, c],
            device_id={"elem": group + 1}, device_id_type=MESH,
        )
        left = pltpu.make_async_remote_copy(
            source(c, 1), halo.at[1, c], send.at[1, c], recv.at[1, c],
            device_id={"elem": group - 1}, device_id_type=MESH,
        )
        return right, left

    def prev_copies(c):
        return halo_copies(lambda c, side: rims.at[side, c], halo_prev, p_send, p_recv, c)

    def first_copies(c):
        def source(c, side):
            return first.at[c, pl.ds((group_elems - rim) * (1 - side), rim)]

        return halo_copies(source, halo_first, f_send, f_recv, c)

    def start_halo(copies):
        right, left = copies
        pl.when(has_right)(right.start)
        pl.when(has_left)(left.start)

    def wait_halo_recv(copies):
        right, left = copies
        pl.when(has_left)(right.wait_recv)
        pl.when(has_right)(left.wait_recv)

    def wait_halo_send(copies):
        right, left = copies
        pl.when(has_right)(right.wait_send)
        pl.when(has_left)(left.wait_send)

    loads[0].wait()

    def gather_rims(c, carry):
        for i in range(rim):
            rims[0, c, i] = prev_rows(c, group_elems - rim + i)
            rims[1, c, i] = prev_rows(c, i)
        return carry

    lax.fori_loop(0, CHUNKS, gather_rims, 0)
    pl.semaphore_wait(
        barrier, modes - 1 + has_left.astype(jnp.int32) + has_right.astype(jnp.int32)
    )

    def send_rims(c, carry):
        start_halo(prev_copies(c))
        return carry

    lax.fori_loop(0, CHUNKS, send_rims, 0)

    def set_weights(ref, at, matrix):
        high, low = split(matrix.T)
        for part in range(2):
            ref[pl.ds(at + part * nodes, nodes), pl.ds(0, nodes)] = high
            ref[pl.ds(at + part * nodes, nodes), pl.ds(nodes, nodes)] = low

    loads[1].wait()
    loads[2].wait()
    set_weights(w_slope, 0, der[...])

    block = min(256, half)
    for e in range(elems):
        for b in range(half // block):
            lower = vel[pl.ds(b * block * elems + e, block, stride=elems), :]
            upper = vel[pl.ds((half + b * block) * elems + e, block, stride=elems), :]
            values = jnp.concatenate([lower, upper], axis=0)
            both = jnp.dot(
                jnp.concatenate(split(values), axis=1), w_slope[...], preferred_element_type=f32
            )
            slope = both[:, :nodes] + both[:, nodes:]
            product = values - dt_step * values * slope
            lower, upper = product[:block], product[block:]
            for parity, value in enumerate((lower + upper, lower - upper)):
                high, low = split(value)
                where = (pl.ds(b * block, block), pl.ds(e * nodes, nodes))
                folded[(parity, 0) + where] = high
                folded[(parity, 1) + where] = low

    loads[3].wait()
    pairs_of_rows = CHUNKS // 2

    def transform(owner, parity):
        data_high, data_low = folded[parity, 0], folded[parity, 1]
        t_high, t_low = table[0, owner, parity], table[1, owner, parity]
        return (
            jnp.dot(t_high, data_high, preferred_element_type=f32)
            + jnp.dot(t_low, data_high, preferred_element_type=f32)
            + jnp.dot(t_high, data_low, preferred_element_type=f32)
        )

    def y_copy(step, c):
        return pltpu.make_async_remote_copy(
            sent.at[step - 1, c], rhs.at[me, c], y_send.at[step - 1, c], y_recv.at[step - 1, c],
            device_id={"mode": lax.rem(me + step, modes)}, device_id_type=MESH,
        )

    for parity in range(2):
        for step in range(1, modes):
            block_rows = transform(lax.rem(me + step, modes), parity)
            for j in range(pairs_of_rows):
                sent[step - 1, 2 * j + parity] = block_rows[j * count : (j + 1) * count]
            if parity == 0:
                y_copy(step, 0).start()

    def send_rows(c, carry):
        for step in range(1, modes):
            y_copy(step, c).start()
        return carry

    lax.fori_loop(1, CHUNKS, send_rows, 0)

    for parity in range(2):
        block_rows = transform(me, parity)
        for j in range(pairs_of_rows):
            rhs[me, 2 * j + parity] = block_rows[j * count : (j + 1) * count]

    loads[4].wait()
    loads[5].wait()
    set_weights(w_apply, 0, stiff[...])
    for f in range(4):
        set_weights(w_apply, 2 * nodes * (f + 1), coup[f])
    eye = lax.broadcasted_iota(jnp.int32, (nodes, nodes), 0) == lax.broadcasted_iota(
        jnp.int32, (nodes, nodes), 1
    )
    diagonal = jnp.sum(jnp.where(eye, stiff[...], 0.0), axis=0, keepdims=True)
    pairs[zero_slot] = jnp.zeros((count, 2 * nodes), bf16)

    def put_pair(slot, value):
        high, low = split(value)
        pairs[slot, :, pl.ds(0, nodes)] = high
        pairs[slot, :, pl.ds(nodes, nodes)] = low

    def apply(own, halo, copies, c):
        for e in range(group_elems):
            put_pair(rim + e, own(c, e))
        wait_halo_recv(copies)

        @pl.when(has_left)
        def _():
            for i in range(rim):
                put_pair(i, halo[0, c, i])

        @pl.when(has_right)
        def _():
            for i in range(rim):
                put_pair(rim + group_elems + i, halo[1, c, i])

        for e in range(group_elems):
            here = pl.ds(e * count, count)
            staged[here, pl.ds(0, 2 * nodes)] = pairs[rim + e]
            for f in range(4):
                n = near[f, e]
                slot = jnp.clip(n - group * group_elems + rim, 0, zero_slot - 1)
                slot = jnp.where(n >= 0, slot, zero_slot)
                staged[here, pl.ds(2 * nodes * (f + 1), 2 * nodes)] = pairs[slot]
        both = jnp.dot(staged[...], w_apply[...], preferred_element_type=f32)
        return both[:, :nodes] + both[:, nodes:]

    def shifts(c):
        places = lax.broadcasted_iota(jnp.int32, (count, nodes), 0)
        row = me * rows + 2 * ((c // 2) * count + places) + c % 2
        wave = jnp.where(row <= half, row, row - half).astype(f32)
        return 4.0 * (wave / half) ** 2

    def relaxed(weight, value, applied, shift, c, e):
        scaling = reac[e] + shift * axial[e]
        inverse = 1.0 / (diagonal + scaling)
        right = rhs[e // elems, c, :, pl.ds((e % elems) * nodes, nodes)]
        part = applied[e * count : (e + 1) * count]
        return value + weight * inverse * (right - (part + scaling * value))

    def first_sweep(c):
        applied = apply(prev_rows, halo_prev, prev_copies(c), c)
        for step in range(1, modes):
            y_copy(step, c).wait_recv()
        shift = shifts(c)
        for e in range(group_elems):
            first[c, e] = relaxed(first_weight, prev_rows(c, e), applied, shift, c, e)
        start_halo(first_copies(c))

    def out_copy(j):
        size = 2 * count * group_elems
        span = pl.ds(j * size, size)
        return pltpu.make_async_copy(outv.at[span], out_hbm.at[span], out_sem.at[j])

    def second_sweep(c):
        applied = apply(lambda c, e: first[c, e], halo_first, first_copies(c), c)
        shift = shifts(c)
        for e in range(group_elems):
            outv[pl.ds(start_row(c) + e, count, stride=2 * group_elems), :] = relaxed(
                second_weight, first[c, e], applied, shift, c, e
            )
        pl.when(c % 2 == 1)(lambda: out_copy(c // 2).start())

    def stage(s, carry):
        pl.when(s < CHUNKS)(lambda: first_sweep(s))
        pl.when(s >= LAG)(lambda: second_sweep(s - LAG))
        return carry

    lax.fori_loop(0, CHUNKS + LAG, stage, 0)

    def finish(c, carry):
        wait_halo_send(prev_copies(c))
        wait_halo_send(first_copies(c))
        for step in range(1, modes):
            y_copy(step, c).wait_send()
        return carry

    lax.fori_loop(0, CHUNKS, finish, 0)

    def finish_out(j, carry):
        out_copy(j).wait()
        return carry

    lax.fori_loop(0, pairs_of_rows, finish_out, 0)


def body(modes, groups, velocity, previous, derivative, stiffness, coupling, reaction, axial_weight, neighbours):
    planes, elems, nodes = velocity.shape
    rows, group_elems, _ = previous.shape
    half = planes // 2
    rim = group_elems // 4
    count = rows // CHUNKS
    tables = jnp.asarray(dft_tables(planes, modes))
    run = functools.partial(kernel, modes, groups, planes, elems, group_elems, rows, nodes)
    anywhere = pl.BlockSpec(memory_space=pl.ANY)
    scalar = pl.BlockSpec(memory_space=pltpu.SMEM)
    dma = pltpu.SemaphoreType.DMA
    out = pl.pallas_call(
        run,
        out_shape=jax.ShapeDtypeStruct((rows * group_elems, nodes), f32),
        in_specs=[anywhere] * 6 + [scalar] * 3,
        out_specs=anywhere,
        scratch_shapes=[
            pltpu.VMEM((planes * elems, nodes), f32),
            pltpu.VMEM((rows * group_elems, nodes), f32),
            pltpu.VMEM(tables.shape, bf16),
            pltpu.VMEM((nodes, nodes), f32),
            pltpu.VMEM((nodes, nodes), f32),
            pltpu.VMEM((4, nodes, nodes), f32),
            pltpu.VMEM((2 * nodes, 2 * nodes), bf16),
            pltpu.VMEM((10 * nodes, 2 * nodes), bf16),
            pltpu.VMEM((2, 2, half, elems * nodes), bf16),
            pltpu.VMEM((modes - 1, CHUNKS, count, elems * nodes), f32),
            pltpu.VMEM((modes, CHUNKS, count, elems * nodes), f32),
            pltpu.VMEM((2, CHUNKS, rim, count, nodes), f32),
            pltpu.VMEM((CHUNKS, group_elems, count, nodes), f32),
            pltpu.VMEM((2, CHUNKS, rim, count, nodes), f32),
            pltpu.VMEM((2, CHUNKS, rim, count, nodes), f32),
            pltpu.VMEM((group_elems + 2 * rim + 1, count, 2 * nodes), bf16),
            pltpu.VMEM((group_elems * count, 10 * nodes), bf16),
            pltpu.VMEM((rows * group_elems, nodes), f32),
            dma((6,)),
            dma((modes - 1, CHUNKS)),
            dma((modes - 1, CHUNKS)),
            dma((2, CHUNKS)),
            dma((2, CHUNKS)),
            dma((2, CHUNKS)),
            dma((2, CHUNKS)),
            dma((CHUNKS // 2,)),
        ],
        compiler_params=pltpu.CompilerParams(
            collective_id=0, has_side_effects=True, vmem_limit_bytes=63 * 1024 * 1024
        ),
        name="advect_helmholtz",
    )(
        velocity.reshape(planes * elems, nodes),
        previous.reshape(rows * group_elems, nodes),
        tables,
        derivative,
        stiffness,
        coupling,
        reaction,
        axial_weight,
        neighbours.T,
    )
    return out.reshape(rows, group_elems, nodes)


def solution(mesh):
    return jax.shard_map(
        functools.partial(body, mesh.shape["mode"], mesh.shape["elem"]),
        mesh=mesh,
        in_specs=(
            P(None, ("elem", "mode"), None),
            P("mode", "elem", None),
            P(),
            P(),
            P(),
            P("elem"),
            P("elem"),
            P("elem", None),
        ),
        out_specs=P("mode", "elem", None),
        check_vma=False,
    )
```

```python
import functools
import math

import jax
import jax.numpy as jnp
import ml_dtypes
import numpy as np
from jax import lax
from jax.experimental import pallas as pl
from jax.experimental.pallas import tpu as pltpu
from jax.sharding import PartitionSpec as P

dt_step = 0.5
first_weight = 0.7
second_weight = 1.1
CHUNKS = 8
LAG = 2
vmem_bytes = 67043328
vmem_spare = 262144
MESH = pl.DeviceIdType.MESH
bf16 = jnp.bfloat16
f32 = jnp.float32


def dft_tables(planes, modes):
    half = planes // 2
    rows = np.arange(planes)
    waves = np.where(rows <= half, rows, rows - half)
    phase = (waves[:, None] * np.arange(half)[None, :]) % planes
    angles = 2.0 * math.pi / planes * phase
    table = np.where((rows <= half)[:, None], np.cos(angles), -np.sin(angles)) * planes ** (-0.5)
    table = table.reshape(modes, planes // modes // 2, 2, half).transpose(0, 2, 1, 3)
    high = table.astype(ml_dtypes.bfloat16)
    low = (table - high.astype(np.float64)).astype(ml_dtypes.bfloat16)
    return np.stack([high, low])


def split(values):
    high = values.astype(bf16)
    low = (values - high.astype(f32)).astype(bf16)
    return high, low


def kernel(
    modes, groups, planes, elems, group_elems, rows, nodes,
    vel_hbm, prev_hbm, table_hbm, der_hbm, stiff_hbm, coup_hbm, reac, axial, near,
    outv,
    vel, prev, table, der, stiff, coup, w_slope, w_apply, folded, sent, rhs, rims, first,
    halo_prev, halo_first, pairs, staged,
    load_sem, lead_send, lead_recv, y_send, y_recv, p_send, p_recv, f_send, f_recv,
):
    half = planes // 2
    rim = group_elems // 4
    count = rows // CHUNKS
    me = lax.axis_index("mode")
    group = lax.axis_index("elem")
    zero_slot = group_elems + 2 * rim

    loads = [
        pltpu.make_async_copy(src, dst, load_sem.at[i])
        for i, (src, dst) in enumerate(
            [
                (vel_hbm, vel), (der_hbm, der), (table_hbm, table), (prev_hbm, prev),
                (stiff_hbm, stiff), (coup_hbm, coup),
            ]
        )
    ]
    for load in loads:
        load.start()

    barrier = pltpu.get_barrier_semaphore()
    for step in range(1, modes):
        pl.semaphore_signal(
            barrier, inc=1, device_id={"mode": lax.rem(me + step, modes)}, device_id_type=MESH
        )
    has_left = group > 0
    has_right = group < groups - 1

    @pl.when(has_left)
    def _():
        pl.semaphore_signal(barrier, inc=1, device_id={"elem": group - 1}, device_id_type=MESH)

    @pl.when(has_right)
    def _():
        pl.semaphore_signal(barrier, inc=1, device_id={"elem": group + 1}, device_id_type=MESH)

    def start_row(c):
        return (2 * (c // 2) * count + c % 2) * group_elems

    def prev_rows(c, e):
        return prev[pl.ds(start_row(c) + e, count, stride=2 * group_elems), :]

    def halo_copies(source, halo, send, recv, c):
        right = pltpu.make_async_remote_copy(
            source(c, 0), halo.at[0, c], send.at[0, c], recv.at[0, c],
            device_id={"elem": group + 1}, device_id_type=MESH,
        )
        left = pltpu.make_async_remote_copy(
            source(c, 1), halo.at[1, c], send.at[1, c], recv.at[1, c],
            device_id={"elem": group - 1}, device_id_type=MESH,
        )
        return right, left

    def prev_copies(c):
        return halo_copies(lambda c, side: rims.at[side, c], halo_prev, p_send, p_recv, c)

    def first_copies(c):
        def source(c, side):
            return first.at[c, pl.ds((group_elems - rim) * (1 - side), rim)]

        return halo_copies(source, halo_first, f_send, f_recv, c)

    def start_halo(copies):
        right, left = copies
        pl.when(has_right)(right.start)
        pl.when(has_left)(left.start)

    def wait_halo_recv(copies):
        right, left = copies
        pl.when(has_left)(right.wait_recv)
        pl.when(has_right)(left.wait_recv)

    def wait_halo_send(copies):
        right, left = copies
        pl.when(has_right)(right.wait_send)
        pl.when(has_left)(left.wait_send)

    def set_weights(ref, at, matrix):
        high, low = split(matrix.T)
        for part in range(2):
            ref[pl.ds(at + part * nodes, nodes), pl.ds(0, nodes)] = high
            ref[pl.ds(at + part * nodes, nodes), pl.ds(nodes, nodes)] = low

    loads[1].wait()
    set_weights(w_slope, 0, der[...])
    loads[0].wait()

    block = min(256, half)

    def advect(e):
        for b in range(half // block):
            lower = vel[pl.ds(b * block * elems + e, block, stride=elems), :]
            upper = vel[pl.ds((half + b * block) * elems + e, block, stride=elems), :]
            values = jnp.concatenate([lower, upper], axis=0)
            both = jnp.dot(
                jnp.concatenate(split(values), axis=1), w_slope[...], preferred_element_type=f32
            )
            slope = both[:, :nodes] + both[:, nodes:]
            product = values - dt_step * values * slope
            lower, upper = product[:block], product[block:]
            for parity, value in enumerate((lower + upper, lower - upper)):
                high, low = split(value)
                where = (pl.ds(b * block, block), pl.ds(e * nodes, nodes))
                folded[(parity, 0) + where] = high
                folded[(parity, 1) + where] = low

    pairs_of_rows = CHUNKS // 2
    lead = max(1, elems // 4)
    lead_span = pl.ds(0, lead * nodes)
    rest_span = pl.ds(lead * nodes, (elems - lead) * nodes)

    def transform(owner, parity, span):
        data_high, data_low = folded[parity, 0, :, span], folded[parity, 1, :, span]
        t_high, t_low = table[0, owner, parity], table[1, owner, parity]
        return (
            jnp.dot(t_high, data_high, preferred_element_type=f32)
            + jnp.dot(t_low, data_high, preferred_element_type=f32)
            + jnp.dot(t_high, data_low, preferred_element_type=f32)
        )

    def put_rows(ref, parity, block_rows, span):
        for j in range(pairs_of_rows):
            ref[2 * j + parity, :, span] = block_rows[j * count : (j + 1) * count]

    def lead_copy(step):
        return pltpu.make_async_remote_copy(
            sent.at[step - 1, :, :, lead_span], rhs.at[me, :, :, lead_span],
            lead_send.at[step - 1], lead_recv.at[step - 1],
            device_id={"mode": lax.rem(me + step, modes)}, device_id_type=MESH,
        )

    def y_copy(step, c):
        return pltpu.make_async_remote_copy(
            sent.at[step - 1, c, :, rest_span], rhs.at[me, c, :, rest_span],
            y_send.at[step - 1, c], y_recv.at[step - 1, c],
            device_id={"mode": lax.rem(me + step, modes)}, device_id_type=MESH,
        )

    for e in range(lead):
        advect(e)
    loads[2].wait()
    for step in range(1, modes):
        for parity in range(2):
            put_rows(
                sent.at[step - 1], parity,
                transform(lax.rem(me + step, modes), parity, lead_span), lead_span,
            )
    pl.semaphore_wait(
        barrier, modes - 1 + has_left.astype(jnp.int32) + has_right.astype(jnp.int32)
    )
    for step in range(1, modes):
        lead_copy(step).start()

    loads[3].wait()

    def gather_rims(c, carry):
        for i in range(rim):
            rims[0, c, i] = prev_rows(c, group_elems - rim + i)
            rims[1, c, i] = prev_rows(c, i)
        return carry

    lax.fori_loop(0, CHUNKS, gather_rims, 0)
    def send_rims(c, carry):
        start_halo(prev_copies(c))
        return carry

    lax.fori_loop(0, CHUNKS, send_rims, 0)
    for e in range(lead, elems):
        advect(e)
    for parity in range(2):
        for step in range(1, modes):
            put_rows(
                sent.at[step - 1], parity,
                transform(lax.rem(me + step, modes), parity, rest_span), rest_span,
            )
            if parity == 0:
                y_copy(step, 0).start()

    def send_rows(c, carry):
        for step in range(1, modes):
            y_copy(step, c).start()
        return carry

    lax.fori_loop(1, CHUNKS, send_rows, 0)

    whole_span = pl.ds(0, elems * nodes)
    for parity in range(2):
        put_rows(rhs.at[me], parity, transform(me, parity, whole_span), whole_span)

    loads[4].wait()
    loads[5].wait()
    set_weights(w_apply, 0, stiff[...])
    for f in range(4):
        set_weights(w_apply, 2 * nodes * (f + 1), coup[f])
    eye = lax.broadcasted_iota(jnp.int32, (nodes, nodes), 0) == lax.broadcasted_iota(
        jnp.int32, (nodes, nodes), 1
    )
    diagonal = jnp.sum(jnp.where(eye, stiff[...], 0.0), axis=0, keepdims=True)
    pairs[zero_slot] = jnp.zeros((count, 2 * nodes), bf16)

    def put_pair(slot, value):
        high, low = split(value)
        pairs[slot, :, pl.ds(0, nodes)] = high
        pairs[slot, :, pl.ds(nodes, nodes)] = low

    def apply(own, halo, copies, c):
        for e in range(group_elems):
            put_pair(rim + e, own(c, e))
        wait_halo_recv(copies)

        @pl.when(has_left)
        def _():
            for i in range(rim):
                put_pair(i, halo[0, c, i])

        @pl.when(has_right)
        def _():
            for i in range(rim):
                put_pair(rim + group_elems + i, halo[1, c, i])

        for e in range(group_elems):
            here = pl.ds(e * count, count)
            staged[here, pl.ds(0, 2 * nodes)] = pairs[rim + e]
            for f in range(4):
                n = near[f, e]
                slot = jnp.clip(n - group * group_elems + rim, 0, zero_slot - 1)
                slot = jnp.where(n >= 0, slot, zero_slot)
                staged[here, pl.ds(2 * nodes * (f + 1), 2 * nodes)] = pairs[slot]
        both = jnp.dot(staged[...], w_apply[...], preferred_element_type=f32)
        return both[:, :nodes] + both[:, nodes:]

    def shifts(c):
        places = lax.broadcasted_iota(jnp.int32, (count, nodes), 0)
        row = me * rows + 2 * ((c // 2) * count + places) + c % 2
        wave = jnp.where(row <= half, row, row - half).astype(f32)
        return 4.0 * (wave / half) ** 2

    def relaxed(weight, value, applied, shift, c, e):
        scaling = reac[e] + shift * axial[e]
        inverse = 1.0 / (diagonal + scaling)
        right = rhs[e // elems, c, :, pl.ds((e % elems) * nodes, nodes)]
        part = applied[e * count : (e + 1) * count]
        return value + weight * inverse * (right - (part + scaling * value))

    def first_sweep(c):
        applied = apply(prev_rows, halo_prev, prev_copies(c), c)
        for step in range(1, modes):
            y_copy(step, c).wait_recv()
        shift = shifts(c)
        outer = [*range(rim), *range(group_elems - rim, group_elems)]
        for e in outer:
            first[c, e] = relaxed(first_weight, prev_rows(c, e), applied, shift, c, e)
        start_halo(first_copies(c))
        for e in range(rim, group_elems - rim):
            first[c, e] = relaxed(first_weight, prev_rows(c, e), applied, shift, c, e)

    def second_sweep(c):
        applied = apply(lambda c, e: first[c, e], halo_first, first_copies(c), c)
        shift = shifts(c)
        for e in range(group_elems):
            outv[pl.ds(start_row(c) + e, count, stride=2 * group_elems), :] = relaxed(
                second_weight, first[c, e], applied, shift, c, e
            )

    for step in range(1, modes):
        lead_copy(step).wait_recv()

    def stage(s, carry):
        pl.when(s < CHUNKS)(lambda: first_sweep(s))
        pl.when(s >= LAG)(lambda: second_sweep(s - LAG))
        return carry

    lax.fori_loop(0, CHUNKS + LAG, stage, 0)

    for step in range(1, modes):
        lead_copy(step).wait_send()

    def finish(c, carry):
        wait_halo_send(prev_copies(c))
        wait_halo_send(first_copies(c))
        for step in range(1, modes):
            y_copy(step, c).wait_send()
        return carry

    lax.fori_loop(0, CHUNKS, finish, 0)


def body(modes, groups, velocity, previous, derivative, stiffness, coupling, reaction, axial_weight, neighbours):
    planes, elems, nodes = velocity.shape
    rows, group_elems, _ = previous.shape
    half = planes // 2
    rim = group_elems // 4
    count = rows // CHUNKS
    tables = jnp.asarray(dft_tables(planes, modes))
    run = functools.partial(kernel, modes, groups, planes, elems, group_elems, rows, nodes)
    anywhere = pl.BlockSpec(memory_space=pltpu.HBM)
    scalar = pl.BlockSpec(memory_space=pltpu.SMEM)
    dma = pltpu.SemaphoreType.DMA
    scratch = [
        pltpu.VMEM((planes * elems, nodes), f32),
        pltpu.VMEM((rows * group_elems, nodes), f32),
        pltpu.VMEM(tables.shape, bf16),
        pltpu.VMEM((nodes, nodes), f32),
        pltpu.VMEM((nodes, nodes), f32),
        pltpu.VMEM((4, nodes, nodes), f32),
        pltpu.VMEM((2 * nodes, 2 * nodes), bf16),
        pltpu.VMEM((10 * nodes, 2 * nodes), bf16),
        pltpu.VMEM((2, 2, half, elems * nodes), bf16),
        pltpu.VMEM((modes - 1, CHUNKS, count, elems * nodes), f32),
        pltpu.VMEM((modes, CHUNKS, count, elems * nodes), f32),
        pltpu.VMEM((2, CHUNKS, rim, count, nodes), f32),
        pltpu.VMEM((CHUNKS, group_elems, count, nodes), f32),
        pltpu.VMEM((2, CHUNKS, rim, count, nodes), f32),
        pltpu.VMEM((2, CHUNKS, rim, count, nodes), f32),
        pltpu.VMEM((group_elems + 2 * rim + 1, count, 2 * nodes), bf16),
        pltpu.VMEM((group_elems * count, 10 * nodes), bf16),
    ]
    semaphores = [
        dma((6,)),
        dma((modes - 1,)),
        dma((modes - 1,)),
        dma((modes - 1, CHUNKS)),
        dma((modes - 1, CHUNKS)),
        dma((2, CHUNKS)),
        dma((2, CHUNKS)),
        dma((2, CHUNKS)),
        dma((2, CHUNKS)),
    ]
    out = pl.pallas_call(
        run,
        out_shape=pltpu.VMEM((rows * group_elems, nodes), f32),
        in_specs=[anywhere] * 6 + [scalar] * 3,
        out_specs=pl.BlockSpec(memory_space=pltpu.VMEM),
        scratch_shapes=scratch + semaphores,
        compiler_params=pltpu.CompilerParams(
            collective_id=0, has_side_effects=True, vmem_limit_bytes=vmem_bytes - 4 * rows * group_elems * nodes - 262144
        ),
        name="advect_helmholtz",
    )(
        velocity.reshape(planes * elems, nodes),
        previous.reshape(rows * group_elems, nodes),
        tables,
        derivative,
        stiffness,
        coupling,
        reaction,
        axial_weight,
        neighbours.T,
    )
    return out.reshape(rows, group_elems, nodes)


def solution(mesh):
    return jax.shard_map(
        functools.partial(body, mesh.shape["mode"], mesh.shape["elem"]),
        mesh=mesh,
        in_specs=(
            P(None, ("elem", "mode"), None),
            P("mode", "elem", None),
            P(),
            P(),
            P(),
            P("elem"),
            P("elem"),
            P("elem", None),
        ),
        out_specs=P("mode", "elem", None),
        check_vma=False,
    )
```
